32 devices in a mesh: grp: 2 (over x), mod: 16 (over z, y, core).
Axes of the slice: x: 2, y: 2, z: 4, core: 2. Of those that a mesh axis runs over, the one named last changes fastest.
Arguments:
- inputs_proj: bfloat16 [128, 16, 1536], P(('grp', 'mod')), parts along dimension 0, may hold values from -2.5 to 2.5
- outputs_proj: bfloat16 [128, 16, 1280], P(('grp', 'mod')), parts along dimension 0, may hold values from -2.5 to 2.5
- lengths: int32 [128], P(('grp', 'mod')), parts along dimension 0, may hold values from 16 to 32, as said below
- owner: int32 [16], replicated, may hold values from 0 to 15, each once
- fisher_inv: bfloat16 [16, 1920, 1920], P('mod'), may hold values from -25 to 25, as said below
- query_grads: bfloat16 [16, 512, 1920], P('mod'), may hold values from -0.03125 to 0.03125
Outputs:
- scores: float32 [128, 512], P(('grp', 'mod')), parts along dimension 0
The draws below stay inside these ranges and needn't reach their ends.
There are 2 independent parts, one for each index of `grp`. The reference program is written for one: setup_inputs(seed, part) draws one part's arguments, and reference() takes and returns one part's arrays. A program takes and returns all parts, laid end to end along the dimension named above; an argument that names none is the same for every part. Nothing has to cross between parts.
Inputs may be any that keep to these rules, and one draw needn't show every extreme that they name: `fisher_inv`: each matrix is symmetric. `lengths`: some example of each group has all 32 slots live.
All inputs are finite; a program needn't handle non-finite values.
Results may differ from the reference program's by a relative error of at most 0.0041.
Values may be sent and summed in bfloat16 or wider, within the bound.
No kernel may reach another device: no remote copies, remote signals or barrier semaphores. Data moves between devices by JAX's collectives and lax.ppermute only.
A program may use at most 128 MiB of HBM per device.

```python
import math
import jax
import jax.numpy as jnp
from jax import lax

OUT_RANK = 40
IN_RANK = 48
GRAD_DIM = 1920
SEQ_LEN = 32
QUERIES = 512
EXAMPLES = 64
MODULES = 16


def draw_lengths(key, part):
    key_len = jax.random.fold_in(key, 21)
    key_full = jax.random.fold_in(key, 22)
    drawn = jax.random.randint(key_len, (EXAMPLES,), SEQ_LEN // 2, SEQ_LEN + 1, dtype=jnp.int32)
    position = jax.random.randint(key_full, (), 0, EXAMPLES, dtype=jnp.int32)
    return jnp.where(jnp.arange(EXAMPLES, dtype=jnp.int32) == position, jnp.int32(SEQ_LEN), drawn)


def draw_fisher_inv(key, part):
    key_diag = jax.random.fold_in(key, 11)
    key_noise = jax.random.fold_in(key, 12)
    size = OUT_RANK * IN_RANK
    diag = jnp.exp(jax.random.uniform(key_diag, (MODULES, size), jnp.float32, math.log(0.5), math.log(2.0)))
    noise = jax.random.normal(key_noise, (MODULES, size, size), jnp.float32)
    noise = jnp.clip((noise + jnp.swapaxes(noise, 1, 2)) / math.sqrt(2.0), -6.0, 6.0)
    matrix = noise * (0.6 / math.sqrt(size)) + diag[:, :, None] * jnp.eye(size, dtype=jnp.float32)[None]
    return matrix.astype(jnp.bfloat16)


def level_of(rng, shape, cuts, smallest, largest):
    def one(dim, parts):
        steps = jax.random.uniform(jax.random.fold_in(jax.random.fold_in(rng, 6), dim), (parts,), jnp.float32, smallest / len(cuts), largest / len(cuts))
        return jnp.repeat(jnp.exp(steps), shape[dim] // parts).reshape((-1,) + (1,) * (len(shape) - dim - 1))

    level = one(*cuts[0])
    for cut in cuts[1:]:
        level = level * one(*cut)
    return level


def scatter_about(rng, shape, width, limit, pieces=(), kind=jnp.bfloat16):
    level = level_of(rng, shape, pieces, -0.22, 0.18) if pieces else 1.0
    result = jax.random.normal(rng, shape, jnp.float32) * width * level
    return jnp.minimum(jnp.maximum(result, -limit), limit).astype(kind)


def setup_inputs(seed: int = 0, part: int = 0) -> dict:
    key_list = jax.random.split(jax.random.key(seed), 7)
    part_keys = jax.random.split(jax.random.fold_in(key_list[6], part), 7)
    inputs_proj = scatter_about(part_keys[0], (EXAMPLES, MODULES, IN_RANK * SEQ_LEN), 0.4, 2.5, ((0, 16),))
    outputs_proj = scatter_about(part_keys[1], (EXAMPLES, MODULES, OUT_RANK * SEQ_LEN), 0.4, 2.5, ((0, 16),))
    lengths = draw_lengths(jax.random.fold_in(jax.random.fold_in(key_list[6], part), 71), part)
    owner = jax.random.permutation(key_list[3], MODULES).astype(jnp.int32)
    fisher_inv = draw_fisher_inv(jax.random.fold_in(key_list[6], 71), part)
    query_grads = scatter_about(key_list[5], (MODULES, QUERIES, GRAD_DIM), (GRAD_DIM * MODULES) ** -0.5, 0.03125, ((0, 16),))
    return dict(inputs_proj=inputs_proj, outputs_proj=outputs_proj, lengths=lengths, owner=owner, fisher_inv=fisher_inv, query_grads=query_grads)


def reference(inputs_proj, outputs_proj, lengths, owner, fisher_inv, query_grads):
    live = jnp.arange(SEQ_LEN, dtype=jnp.int32)[None, :] < lengths[:, None]
    live_in = jnp.where(live[:, None, None, :], inputs_proj.reshape(EXAMPLES, MODULES, IN_RANK, SEQ_LEN), jnp.zeros((), inputs_proj.dtype))
    live_out = jnp.where(live[:, None, None, :], outputs_proj.reshape(EXAMPLES, MODULES, OUT_RANK, SEQ_LEN), jnp.zeros((), outputs_proj.dtype))

    def one_module(total, index):
        feat_in = lax.dynamic_index_in_dim(live_in, index, 1, keepdims=False).astype(jnp.float32)
        feat_out = lax.dynamic_index_in_dim(live_out, index, 1, keepdims=False).astype(jnp.float32)
        grads = jnp.einsum("eol,eil->eoi", feat_out, feat_in).astype(jnp.bfloat16).reshape(EXAMPLES, OUT_RANK * IN_RANK)
        slot = owner[index]
        query_slot = lax.dynamic_index_in_dim(query_grads, slot, 0, keepdims=False)
        fisher_slot = lax.dynamic_index_in_dim(fisher_inv, slot, 0, keepdims=False)
        precond = jnp.dot(query_slot, fisher_slot, preferred_element_type=jnp.float32).astype(jnp.bfloat16)
        return total + jnp.dot(grads, precond.T, preferred_element_type=jnp.float32), None

    scores, _ = lax.scan(one_module, jnp.zeros((EXAMPLES, QUERIES), jnp.float32), jnp.arange(MODULES, dtype=jnp.int32))
    return scores
```

```python
import jax
import jax.numpy as jnp
from jax import lax
from jax.sharding import PartitionSpec as P

OUT_RANK = 40
IN_RANK = 48
SEQ_LEN = 32


def masked(source, lengths, features):
    count_rows = source.shape[0]
    count_modules = source.shape[1]
    live = (lax.broadcasted_iota(jnp.int32, (count_rows, SEQ_LEN), 1) < lengths[:, None]).astype(
        source.dtype
    )
    return source.reshape(count_rows, count_modules, features, SEQ_LEN) * live[:, None, None, :]


def outer_grads(side_out, side_in):
    formed = jnp.einsum("emol,emil->emoi", side_out, side_in, preferred_element_type=jnp.float32)
    return formed.astype(jnp.bfloat16)


def local(inputs_proj, outputs_proj, lengths, owner, fisher_inv, query_grads):
    count_modules = owner.shape[0]
    local_rows = inputs_proj.shape[0]
    local_in = masked(inputs_proj, lengths, IN_RANK)
    local_out = masked(outputs_proj, lengths, OUT_RANK)
    inverse = (
        jnp.zeros((count_modules,), jnp.int32)
        .at[owner]
        .set(jnp.arange(count_modules, dtype=jnp.int32))
    )
    precond = jnp.dot(query_grads[0], fisher_inv[0], preferred_element_type=jnp.float32).astype(
        jnp.bfloat16
    )
    formed = outer_grads(local_out, local_in).reshape(local_rows, count_modules, OUT_RANK * IN_RANK)
    routed = jnp.take(formed, inverse, axis=1)
    received = lax.all_to_all(routed, "mod", split_axis=1, concat_axis=0, tiled=True)
    example_grads = received.reshape(received.shape[0], OUT_RANK * IN_RANK)
    partial = lax.dot_general(
        example_grads, precond, (((1,), (1,)), ((), ())), preferred_element_type=jnp.float32
    )
    spread = lax.all_to_all(
        partial.reshape(count_modules, local_rows, partial.shape[1]),
        "mod",
        split_axis=0,
        concat_axis=0,
        tiled=True,
    )
    return jnp.sum(spread, axis=0)


def solution(mesh):
    return jax.shard_map(
        local,
        mesh=mesh,
        in_specs=(
            P(("grp", "mod"), None, None),
            P(("grp", "mod"), None, None),
            P(("grp", "mod")),
            P(),
            P("mod", None, None),
            P("mod", None, None),
        ),
        out_specs=P(("grp", "mod"), None),
        check_vma=False,
    )
```

```python
import functools

import jax
import jax.numpy as jnp
from jax import lax
from jax.experimental import pallas as pl
from jax.experimental.pallas import tpu as pltpu
from jax.sharding import PartitionSpec as P

OUT_RANK = 40
IN_RANK = 48
SEQ_LEN = 32
LANES = 128
HALF = LANES // 2
HALF_OUT = OUT_RANK // 2
BLOCK_OUT = 5


def form_kernel(examples, modules, owner_ref, lengths_ref, in_ref, out_ref, grads_ref, in_t, out_t, formed):
    rows = examples * modules
    slots = HALF // examples
    base = pl.program_id(0) * slots

    lane = lax.broadcasted_iota(jnp.int32, (modules, LANES), 1)
    module = lax.broadcasted_iota(jnp.int32, (modules, LANES), 0)
    slot = base + (lane % HALF) // examples
    held = lax.fori_loop(
        0, modules, lambda m, own: jnp.where(module == m, owner_ref[m], own), jnp.zeros_like(lane), unroll=modules <= 16
    )
    match = held == slot
    picks = [jnp.where(match & (lane % examples == e), 1.0, 0.0) for e in range(examples)]
    pick = jnp.concatenate(picks, axis=0)
    row_lane = lax.broadcasted_iota(jnp.int32, (rows, LANES), 1)
    low = jnp.where(row_lane < HALF, pick, 0.0).astype(jnp.bfloat16)
    high = jnp.where(row_lane >= HALF, pick, 0.0).astype(jnp.bfloat16)
    pick = pick.astype(jnp.bfloat16)

    over_rows = (((0,), (0,)), ((), ()))
    half_cols = HALF_OUT * SEQ_LEN
    in_t[...] = lax.dot_general(in_ref[...], pick, over_rows, preferred_element_type=jnp.float32)
    turned = lax.dot_general(
        out_ref[:, :half_cols], low, over_rows, preferred_element_type=jnp.float32
    ) + lax.dot_general(out_ref[:, half_cols:], high, over_rows, preferred_element_type=jnp.float32)

    example = lax.broadcasted_iota(jnp.int32, (half_cols, LANES), 1) % examples
    live = jnp.zeros((half_cols, LANES), jnp.int32)
    for e in range(examples):
        live = jnp.where(example == e, lengths_ref[e], live)
    slot_t = lax.broadcasted_iota(jnp.int32, (half_cols, LANES), 0) % SEQ_LEN
    out_t[...] = jnp.where(slot_t < live, turned, 0.0)

    @pl.loop(0, HALF_OUT // BLOCK_OUT)
    def _(block):
        first = block * (BLOCK_OUT * SEQ_LEN)
        sums = [jnp.zeros((IN_RANK, LANES), jnp.float32) for _ in range(BLOCK_OUT)]
        for t in range(SEQ_LEN):
            features = in_t[pl.ds(t, IN_RANK, stride=SEQ_LEN), :]
            for k in range(BLOCK_OUT):
                sums[k] = sums[k] + features * out_t[pl.ds(first + k * SEQ_LEN + t, 1), :]
        start = pl.multiple_of(block * (BLOCK_OUT * IN_RANK), BLOCK_OUT * IN_RANK)
        formed[pl.ds(start, BLOCK_OUT * IN_RANK), :] = jnp.concatenate(sums, axis=0).astype(jnp.bfloat16)

    turned_back = formed[...].T
    grads_ref[...] = jnp.concatenate([turned_back[:HALF], turned_back[HALF:]], axis=1)


def form_grads(inputs_proj, outputs_proj, lengths, owner):
    examples, modules, in_cols = inputs_proj.shape
    out_cols = outputs_proj.shape[2]
    rows = examples * modules
    return pl.pallas_call(
        functools.partial(form_kernel, examples, modules),
        out_shape=jax.ShapeDtypeStruct((rows, OUT_RANK * IN_RANK), jnp.bfloat16),
        grid=(rows // HALF,),
        in_specs=[
            pl.BlockSpec(memory_space=pltpu.SMEM),
            pl.BlockSpec(memory_space=pltpu.SMEM),
            pl.BlockSpec((rows, in_cols), lambda i: (0, 0)),
            pl.BlockSpec((rows, out_cols), lambda i: (0, 0)),
        ],
        out_specs=pl.BlockSpec((HALF, OUT_RANK * IN_RANK), lambda i: (i, 0)),
        scratch_shapes=[
            pltpu.VMEM((in_cols, LANES), jnp.float32),
            pltpu.VMEM((HALF_OUT * SEQ_LEN, LANES), jnp.float32),
            pltpu.VMEM((HALF_OUT * IN_RANK, LANES), jnp.bfloat16),
        ],
        compiler_params=pltpu.CompilerParams(vmem_limit_bytes=24 << 20),
    )(owner, lengths, inputs_proj.reshape(rows, in_cols), outputs_proj.reshape(rows, out_cols))


def score_kernel(grads_ref, fisher_ref, query_ref, scores_ref, total):
    step = pl.program_id(0)

    @pl.when(step == 0)
    def _():
        total[...] = jnp.zeros_like(total)

    solved = jnp.dot(grads_ref[...], fisher_ref[...], preferred_element_type=jnp.float32)
    main = solved.astype(jnp.bfloat16)
    rest = (solved - main.astype(jnp.float32)).astype(jnp.bfloat16)
    rows = main.shape[0]
    both = lax.dot_general(
        jnp.concatenate([main, rest], axis=0),
        query_ref[...],
        (((1,), (1,)), ((), ())),
        preferred_element_type=jnp.float32,
    )
    total[...] += both[:rows] + both[rows:]

    @pl.when(step == pl.num_programs(0) - 1)
    def _():
        scores_ref[...] = total[...].astype(scores_ref.dtype)


def module_scores(grads, fisher, query, columns=384):
    rows, size = grads.shape
    queries = query.shape[0]
    return pl.pallas_call(
        score_kernel,
        out_shape=jax.ShapeDtypeStruct((rows, queries), jnp.bfloat16),
        grid=(size // columns,),
        in_specs=[
            pl.BlockSpec((rows, size), lambda i: (0, 0)),
            pl.BlockSpec((size, columns), lambda i: (0, i)),
            pl.BlockSpec((queries, columns), lambda i: (0, i)),
        ],
        out_specs=pl.BlockSpec((rows, queries), lambda i: (0, 0)),
        scratch_shapes=[pltpu.VMEM((rows, queries), jnp.float32)],
        compiler_params=pltpu.CompilerParams(vmem_limit_bytes=32 << 20),
    )(grads, fisher, query)


def local(inputs_proj, outputs_proj, lengths, owner, fisher_inv, query_grads):
    routed = form_grads(inputs_proj, outputs_proj, lengths, owner)
    received = lax.all_to_all(routed, "mod", split_axis=0, concat_axis=0, tiled=True)
    partial = module_scores(received, fisher_inv[0], query_grads[0])
    spread = lax.all_to_all(partial, "mod", split_axis=0, concat_axis=0, tiled=True)
    groups = spread.reshape(owner.shape[0], inputs_proj.shape[0], spread.shape[1])
    return jnp.sum(groups.astype(jnp.float32), axis=0)


def solution(mesh):
    return jax.shard_map(
        local,
        mesh=mesh,
        in_specs=(
            P(("grp", "mod"), None, None),
            P(("grp", "mod"), None, None),
            P(("grp", "mod")),
            P(),
            P("mod", None, None),
            P("mod", None, None),
        ),
        out_specs=P(("grp", "mod"), None),
        check_vma=False,
    )
```

```python
import functools

import jax
import jax.numpy as jnp
from jax import lax
from jax.experimental import pallas as pl
from jax.experimental.pallas import tpu as pltpu
from jax.sharding import PartitionSpec as P

OUT_RANK = 40
IN_RANK = 48
SEQ_LEN = 32
LANES = 128
HALF = LANES // 2
HALF_OUT = OUT_RANK // 2
BLOCK_OUT = 5
LONG = pl.CostEstimate(flops=20_000_000_000, bytes_accessed=30_000_000, transcendentals=0)


def form_kernel(
    examples, modules, owner_hbm, lengths_hbm, in_hbm, out_hbm, grads_ref,
    owner_ref, lengths_ref, in_ref, out_ref, in_t, out_t, formed, arrived,
):
    rows = examples * modules
    pairs = ((owner_hbm, owner_ref), (lengths_hbm, lengths_ref), (in_hbm, in_ref), (out_hbm, out_ref))
    copies = [pltpu.make_async_copy(there, here, arrived.at[k]) for k, (there, here) in enumerate(pairs)]

    @pl.when(pl.program_id(0) == 0)
    def _():
        for copy in copies:
            copy.start()
        for copy in copies:
            copy.wait()

    slots = HALF // examples
    base = pl.program_id(0) * slots

    lane = lax.broadcasted_iota(jnp.int32, (modules, LANES), 1)
    module = lax.broadcasted_iota(jnp.int32, (modules, LANES), 0)
    slot = base + (lane % HALF) // examples
    held = lax.fori_loop(
        0, modules, lambda m, own: jnp.where(module == m, owner_ref[m], own), jnp.zeros_like(lane), unroll=modules <= 16
    )
    match = held == slot
    picks = [jnp.where(match & (lane % examples == e), 1.0, 0.0) for e in range(examples)]
    pick = jnp.concatenate(picks, axis=0)
    row_lane = lax.broadcasted_iota(jnp.int32, (rows, LANES), 1)
    low = jnp.where(row_lane < HALF, pick, 0.0).astype(jnp.bfloat16)
    high = jnp.where(row_lane >= HALF, pick, 0.0).astype(jnp.bfloat16)
    pick = pick.astype(jnp.bfloat16)

    over_rows = (((0,), (0,)), ((), ()))
    half_cols = HALF_OUT * SEQ_LEN
    in_t[...] = lax.dot_general(in_ref[...], pick, over_rows, preferred_element_type=jnp.float32)
    turned = lax.dot_general(
        out_ref[:, :half_cols], low, over_rows, preferred_element_type=jnp.float32
    ) + lax.dot_general(out_ref[:, half_cols:], high, over_rows, preferred_element_type=jnp.float32)

    example = lax.broadcasted_iota(jnp.int32, (half_cols, LANES), 1) % examples
    live = jnp.zeros((half_cols, LANES), jnp.int32)
    for e in range(examples):
        live = jnp.where(example == e, lengths_ref[e], live)
    slot_t = lax.broadcasted_iota(jnp.int32, (half_cols, LANES), 0) % SEQ_LEN
    out_t[...] = jnp.where(slot_t < live, turned, 0.0)

    @pl.loop(0, HALF_OUT // BLOCK_OUT)
    def _(block):
        first = block * (BLOCK_OUT * SEQ_LEN)
        sums = [jnp.zeros((IN_RANK, LANES), jnp.float32) for _ in range(BLOCK_OUT)]
        for t in range(SEQ_LEN):
            features = in_t[pl.ds(t, IN_RANK, stride=SEQ_LEN), :]
            for k in range(BLOCK_OUT):
                sums[k] = sums[k] + features * out_t[pl.ds(first + k * SEQ_LEN + t, 1), :]
        start = pl.multiple_of(block * (BLOCK_OUT * IN_RANK), BLOCK_OUT * IN_RANK)
        formed[pl.ds(start, BLOCK_OUT * IN_RANK), :] = jnp.concatenate(sums, axis=0).astype(jnp.bfloat16)

    turned_back = formed[...].T
    grads = jnp.concatenate([turned_back[:HALF], turned_back[HALF:]], axis=1)
    grads_ref[...] = grads.reshape(grads_ref.shape)


def form_grads(inputs_proj, outputs_proj, lengths, owner):
    examples, modules, in_cols = inputs_proj.shape
    out_cols = outputs_proj.shape[2]
    rows = examples * modules
    operands = (owner, lengths, inputs_proj.reshape(rows, in_cols), outputs_proj.reshape(rows, out_cols))
    return pl.pallas_call(
        functools.partial(form_kernel, examples, modules),
        out_shape=jax.ShapeDtypeStruct((modules, examples, OUT_RANK * IN_RANK), jnp.bfloat16),
        grid=(rows // HALF,),
        in_specs=[pl.BlockSpec(memory_space=pltpu.HBM)] * 4,
        out_specs=pl.BlockSpec((HALF // examples, examples, OUT_RANK * IN_RANK), lambda i: (i, 0, 0)),
        scratch_shapes=[
            pltpu.SMEM((modules,), jnp.int32),
            pltpu.SMEM((examples,), jnp.int32),
            pltpu.VMEM((rows, in_cols), jnp.bfloat16),
            pltpu.VMEM((rows, out_cols), jnp.bfloat16),
            pltpu.VMEM((in_cols, LANES), jnp.float32),
            pltpu.VMEM((HALF_OUT * SEQ_LEN, LANES), jnp.float32),
            pltpu.VMEM((HALF_OUT * IN_RANK, LANES), jnp.bfloat16),
            pltpu.SemaphoreType.DMA((4,)),
        ],
        compiler_params=pltpu.CompilerParams(vmem_limit_bytes=24 << 20),
        cost_estimate=LONG,
    )(*[pltpu.with_memory_space_constraint(x, pltpu.HBM) for x in operands])


def score_kernel(grads_ref, fisher_ref, query_ref, scores_ref):
    slots, examples, size = grads_ref.shape
    grads = grads_ref[...].reshape(slots * examples, size)
    solved = jnp.dot(grads, fisher_ref[0], preferred_element_type=jnp.float32)
    main = solved.astype(jnp.bfloat16)
    rest = (solved - main.astype(jnp.float32)).astype(jnp.bfloat16)
    rows = main.shape[0]
    both = lax.dot_general(
        jnp.concatenate([main, rest], axis=0),
        query_ref[0],
        (((1,), (1,)), ((), ())),
        preferred_element_type=jnp.float32,
    )
    scores_ref[...] = (both[:rows] + both[rows:]).astype(scores_ref.dtype).reshape(scores_ref.shape)


def module_scores(grads, fisher, query):
    slots, examples, _ = grads.shape
    return pl.pallas_call(
        score_kernel,
        out_shape=jax.ShapeDtypeStruct((slots, examples, query.shape[1]), jnp.bfloat16),
        in_specs=[pl.BlockSpec(memory_space=pltpu.VMEM)] * 3,
        out_specs=pl.BlockSpec(memory_space=pltpu.VMEM),
        compiler_params=pltpu.CompilerParams(vmem_limit_bytes=16 << 20),
        cost_estimate=pl.CostEstimate(
            flops=2 * slots * examples * (fisher.size + 2 * query.size),
            bytes_accessed=2 * (fisher.size + query.size),
            transcendentals=0,
        ),
    )(grads, fisher, query)


def local(inputs_proj, outputs_proj, lengths, owner, fisher_inv, query_grads):
    routed = form_grads(inputs_proj, outputs_proj, lengths, owner)
    received = lax.all_to_all(routed, "mod", split_axis=0, concat_axis=0, tiled=True)
    partial = module_scores(received, fisher_inv, query_grads)
    spread = lax.all_to_all(partial, "mod", split_axis=0, concat_axis=0, tiled=True)
    return jnp.sum(spread.astype(jnp.float32), axis=0)


def solution(mesh):
    return jax.shard_map(
        local,
        mesh=mesh,
        in_specs=(
            P(("grp", "mod"), None, None),
            P(("grp", "mod"), None, None),
            P(("grp", "mod")),
            P(),
            P("mod", None, None),
            P("mod", None, None),
        ),
        out_specs=P(("grp", "mod"), None),
        check_vma=False,
    )
```

```python
import functools

import jax
import jax.numpy as jnp
from jax import lax
from jax.experimental import pallas as pl
from jax.experimental.pallas import tpu as pltpu
from jax.sharding import PartitionSpec as P

OUT_RANK = 40
IN_RANK = 48
SEQ_LEN = 32
LANES = 128
HALF = LANES // 2
HALF_OUT = OUT_RANK // 2
BLOCK_IN = 16
PITCH = SEQ_LEN + 8
LONG = pl.CostEstimate(flops=20_000_000_000, bytes_accessed=30_000_000, transcendentals=0)


def form_kernel(
    examples, owner_hbm, lengths_hbm, in_hbm, out_hbm, grads_ref,
    owner_ref, lengths_ref, in_ref, out_ref, in_t, out_t, formed, arrived,
):
    modules = HALF // examples
    here = pl.ds(pl.program_id(0) * modules, modules)
    pairs = (
        (in_hbm.at[:, here], in_ref),
        (out_hbm.at[:, here], out_ref),
        (lengths_hbm, lengths_ref),
        (owner_hbm, owner_ref),
    )
    copies = [pltpu.make_async_copy(there, mine, arrived.at[k]) for k, (there, mine) in enumerate(pairs)]
    for copy in copies:
        copy.start()
    for copy in copies:
        copy.wait()

    half_cols = HALF_OUT * SEQ_LEN
    inputs = in_ref[...].reshape(HALF, in_ref.shape[2])
    outputs = out_ref[...].reshape(HALF, out_ref.shape[2])
    turned_in = jnp.concatenate([inputs, inputs], axis=0).T.astype(jnp.float32)
    for i in range(IN_RANK):
        in_t[pl.ds(i * PITCH, SEQ_LEN), :] = turned_in[i * SEQ_LEN : (i + 1) * SEQ_LEN]
    turned = jnp.concatenate([outputs[:, :half_cols], outputs[:, half_cols:]], axis=0).T.astype(jnp.float32)

    example = lax.broadcasted_iota(jnp.int32, (half_cols, LANES), 1) % HALF // modules
    live = jnp.zeros((half_cols, LANES), jnp.int32)
    for e in range(examples):
        live = jnp.where(example == e, lengths_ref[e], live)
    slot_t = lax.broadcasted_iota(jnp.int32, (half_cols, LANES), 0) % SEQ_LEN
    out_t[...] = jnp.where(slot_t < live, turned, 0.0)

    @pl.loop(0, IN_RANK // BLOCK_IN)
    def _(block):
        first = block * (BLOCK_IN * PITCH)
        sums = [jnp.zeros((BLOCK_IN, LANES), jnp.float32) for _ in range(HALF_OUT)]
        for t in range(SEQ_LEN):
            features = in_t[pl.ds(first + t, BLOCK_IN, stride=PITCH), :]
            for o in range(HALF_OUT):
                sums[o] = sums[o] + features * out_t[pl.ds(o * SEQ_LEN + t, 1), :]
        for o in range(HALF_OUT):
            start = pl.multiple_of(o * IN_RANK + block * BLOCK_IN, BLOCK_IN)
            formed[pl.ds(start, BLOCK_IN), :] = sums[o].astype(jnp.bfloat16)

    row = lax.broadcasted_iota(jnp.int32, (HALF, HALF), 0)
    lane = lax.broadcasted_iota(jnp.int32, (HALF, HALF), 1)
    pick = jnp.where(lane == row % examples * modules + row // examples, 1.0, 0.0).astype(jnp.bfloat16)
    blank = jnp.zeros_like(pick)
    low = jnp.concatenate([pick, blank], axis=1)
    high = jnp.concatenate([blank, pick], axis=1)

    def take(side, first, last):
        return lax.dot_general(side, formed[first:last], (((1,), (1,)), ((), ())), preferred_element_type=jnp.float32)

    half = HALF_OUT * IN_RANK
    whole = half // LANES * LANES
    parts = [take(low, 0, whole)]
    if whole < half:
        edge = jnp.concatenate([formed[whole:half], formed[: whole + LANES - half]], axis=0)
        upper = lax.broadcasted_iota(jnp.int32, (HALF, LANES), 1) >= half - whole
        over_lanes = (((1,), (1,)), ((), ()))
        parts.append(
            jnp.where(
                upper,
                lax.dot_general(high, edge, over_lanes, preferred_element_type=jnp.float32),
                lax.dot_general(low, edge, over_lanes, preferred_element_type=jnp.float32),
            )
        )
        parts.append(take(high, whole + LANES - half, half))
    else:
        parts.append(take(high, 0, half))
    grads = jnp.concatenate(parts, axis=1).astype(jnp.bfloat16)
    for m in range(modules):
        slot = owner_ref[pl.program_id(0) * modules + m]
        grads_ref[slot] = grads[m * examples : (m + 1) * examples]


def form_grads(inputs_proj, outputs_proj, lengths, owner):
    examples, modules, in_cols = inputs_proj.shape
    out_cols = outputs_proj.shape[2]
    step = HALF // examples
    shape = (modules, examples, OUT_RANK * IN_RANK)
    operands = (owner, lengths, inputs_proj, outputs_proj)
    return pl.pallas_call(
        functools.partial(form_kernel, examples),
        out_shape=jax.ShapeDtypeStruct(shape, jnp.bfloat16),
        grid=(modules // step,),
        in_specs=[pl.BlockSpec(memory_space=pltpu.HBM)] * 4,
        out_specs=pl.BlockSpec(shape, lambda i: (0, 0, 0)),
        scratch_shapes=[
            pltpu.SMEM((modules,), jnp.int32),
            pltpu.SMEM((examples,), jnp.int32),
            pltpu.VMEM((examples, step, in_cols), jnp.bfloat16),
            pltpu.VMEM((examples, step, out_cols), jnp.bfloat16),
            pltpu.VMEM((IN_RANK * PITCH, LANES), jnp.float32),
            pltpu.VMEM((HALF_OUT * SEQ_LEN, LANES), jnp.float32),
            pltpu.VMEM((HALF_OUT * IN_RANK, LANES), jnp.bfloat16),
            pltpu.SemaphoreType.DMA((4,)),
        ],
        compiler_params=pltpu.CompilerParams(vmem_limit_bytes=24 << 20),
        cost_estimate=LONG,
    )(*[pltpu.with_memory_space_constraint(x, pltpu.HBM) for x in operands])


def score_kernel(grads_ref, fisher_ref, query_ref, scores_ref):
    slots, examples, size = grads_ref.shape
    grads = grads_ref[...].reshape(slots * examples, size)
    solved = jnp.dot(grads, fisher_ref[0], preferred_element_type=jnp.float32)
    main = solved.astype(jnp.bfloat16)
    rest = (solved - main.astype(jnp.float32)).astype(jnp.bfloat16)
    rows = main.shape[0]
    both = lax.dot_general(
        jnp.concatenate([main, rest], axis=0),
        query_ref[0],
        (((1,), (1,)), ((), ())),
        preferred_element_type=jnp.float32,
    )
    scores_ref[...] = (both[:rows] + both[rows:]).astype(scores_ref.dtype).reshape(scores_ref.shape)


def module_scores(grads, fisher, query):
    slots, examples, _ = grads.shape
    return pl.pallas_call(
        score_kernel,
        out_shape=jax.ShapeDtypeStruct((slots, examples, query.shape[1]), jnp.bfloat16),
        in_specs=[pl.BlockSpec(memory_space=pltpu.VMEM)] * 3,
        out_specs=pl.BlockSpec(memory_space=pltpu.VMEM),
        compiler_params=pltpu.CompilerParams(vmem_limit_bytes=16 << 20),
        cost_estimate=pl.CostEstimate(
            flops=2 * slots * examples * (fisher.size + 2 * query.size),
            bytes_accessed=2 * (fisher.size + query.size),
            transcendentals=0,
        ),
    )(grads, fisher, query)


def local(inputs_proj, outputs_proj, lengths, owner, fisher_inv, query_grads):
    routed = form_grads(inputs_proj, outputs_proj, lengths, owner)
    received = lax.all_to_all(routed, "mod", split_axis=0, concat_axis=0, tiled=True)
    partial = module_scores(received, fisher_inv, query_grads)
    spread = lax.all_to_all(partial, "mod", split_axis=0, concat_axis=0, tiled=True)
    return jnp.sum(spread.astype(jnp.float32), axis=0)


def solution(mesh):
    return jax.shard_map(
        local,
        mesh=mesh,
        in_specs=(
            P(("grp", "mod"), None, None),
            P(("grp", "mod"), None, None),
            P(("grp", "mod")),
            P(),
            P("mod", None, None),
            P("mod", None, None),
        ),
        out_specs=P(("grp", "mod"), None),
        check_vma=False,
    )
```

```python
import functools

import jax
import jax.numpy as jnp
from jax import lax
from jax.experimental import pallas as pl
from jax.experimental.pallas import tpu as pltpu
from jax.sharding import PartitionSpec as P

OUT_RANK = 40
IN_RANK = 48
SEQ_LEN = 32
LANES = 128
HALF = LANES // 2
MXU = 256
HALF_OUT = OUT_RANK // 2
BLOCK_IN = 16
PITCH = SEQ_LEN + 4
LONG = pl.CostEstimate(flops=20_000_000_000, bytes_accessed=30_000_000, transcendentals=0)


def form_kernel(
    examples, owner_hbm, lengths_hbm, in_hbm, out_hbm, grads_ref,
    owner_ref, lengths_ref, in_ref, out_ref, in_t, out_t, formed, arrived,
):
    modules = HALF // examples
    here = pl.ds(pl.program_id(0) * modules, modules)
    pairs = (
        (in_hbm.at[:, here], in_ref),
        (out_hbm.at[:, here], out_ref),
        (lengths_hbm, lengths_ref),
        (owner_hbm, owner_ref),
    )
    copies = [pltpu.make_async_copy(there, mine, arrived.at[k]) for k, (there, mine) in enumerate(pairs)]
    for copy in copies:
        copy.start()
    for copy in copies:
        copy.wait()

    half_cols = HALF_OUT * SEQ_LEN
    inputs = in_ref[...].reshape(HALF, in_ref.shape[2])
    outputs = out_ref[...].reshape(HALF, out_ref.shape[2])
    turned_in = jnp.concatenate([inputs, inputs], axis=0).T.astype(jnp.float32)
    for i in range(IN_RANK):
        in_t[pl.ds(i * PITCH, SEQ_LEN), :] = turned_in[i * SEQ_LEN : (i + 1) * SEQ_LEN]
    turned = jnp.concatenate([outputs[:, :half_cols], outputs[:, half_cols:]], axis=0).T.astype(jnp.float32)

    example = lax.broadcasted_iota(jnp.int32, (half_cols, LANES), 1) % HALF // modules
    live = jnp.zeros((half_cols, LANES), jnp.int32)
    for e in range(examples):
        live = jnp.where(example == e, lengths_ref[e], live)
    slot_t = lax.broadcasted_iota(jnp.int32, (half_cols, LANES), 0) % SEQ_LEN
    out_t[...] = jnp.where(slot_t < live, turned, 0.0)

    @pl.loop(0, IN_RANK // BLOCK_IN)
    def _(block):
        first = block * (BLOCK_IN * PITCH)
        sums = [jnp.zeros((BLOCK_IN, LANES), jnp.float32) for _ in range(HALF_OUT)]
        for t in range(SEQ_LEN):
            features = in_t[pl.ds(first + t, BLOCK_IN, stride=PITCH), :]
            for o in range(HALF_OUT):
                sums[o] = sums[o] + features * out_t[pl.ds(o * SEQ_LEN + t, 1), :]
        for o in range(HALF_OUT):
            start = pl.multiple_of(o * IN_RANK + block * BLOCK_IN, BLOCK_IN)
            formed[pl.ds(start, BLOCK_IN), :] = sums[o].astype(jnp.bfloat16)

    row = lax.broadcasted_iota(jnp.int32, (HALF, HALF), 0)
    lane = lax.broadcasted_iota(jnp.int32, (HALF, HALF), 1)
    pick = jnp.where(lane == row % examples * modules + row // examples, 1.0, 0.0).astype(jnp.bfloat16)
    blank = jnp.zeros_like(pick)
    low = jnp.concatenate([pick, blank], axis=1)
    high = jnp.concatenate([blank, pick], axis=1)

    def take(side, first, last):
        return lax.dot_general(side, formed[first:last], (((1,), (1,)), ((), ())), preferred_element_type=jnp.float32)

    half = HALF_OUT * IN_RANK
    whole = half // LANES * LANES
    parts = [take(low, 0, whole)]
    if whole < half:
        edge = jnp.concatenate([formed[whole:half], formed[: whole + LANES - half]], axis=0)
        upper = lax.broadcasted_iota(jnp.int32, (HALF, LANES), 1) >= half - whole
        over_lanes = (((1,), (1,)), ((), ()))
        parts.append(
            jnp.where(
                upper,
                lax.dot_general(high, edge, over_lanes, preferred_element_type=jnp.float32),
                lax.dot_general(low, edge, over_lanes, preferred_element_type=jnp.float32),
            )
        )
        parts.append(take(high, whole + LANES - half, half))
    else:
        parts.append(take(high, 0, half))
    grads = jnp.concatenate(parts, axis=1).astype(jnp.bfloat16)
    for m in range(modules):
        slot = owner_ref[pl.program_id(0) * modules + m]
        grads_ref[slot] = grads[m * examples : (m + 1) * examples]


def form_grads(inputs_proj, outputs_proj, lengths, owner):
    examples, modules, in_cols = inputs_proj.shape
    out_cols = outputs_proj.shape[2]
    step = HALF // examples
    shape = (modules, examples, OUT_RANK * IN_RANK)
    operands = (owner, lengths, inputs_proj, outputs_proj)
    return pl.pallas_call(
        functools.partial(form_kernel, examples),
        out_shape=jax.ShapeDtypeStruct(shape, jnp.bfloat16),
        grid=(modules // step,),
        in_specs=[pl.BlockSpec(memory_space=pltpu.HBM)] * 4,
        out_specs=pl.BlockSpec(shape, lambda i: (0, 0, 0)),
        scratch_shapes=[
            pltpu.SMEM((modules,), jnp.int32),
            pltpu.SMEM((examples,), jnp.int32),
            pltpu.VMEM((examples, step, in_cols), jnp.bfloat16),
            pltpu.VMEM((examples, step, out_cols), jnp.bfloat16),
            pltpu.VMEM((IN_RANK * PITCH, LANES), jnp.float32),
            pltpu.VMEM((HALF_OUT * SEQ_LEN, LANES), jnp.float32),
            pltpu.VMEM((HALF_OUT * IN_RANK, LANES), jnp.bfloat16),
            pltpu.SemaphoreType.DMA((4,)),
        ],
        compiler_params=pltpu.CompilerParams(vmem_limit_bytes=24 << 20),
        cost_estimate=LONG,
    )(*[pltpu.with_memory_space_constraint(x, pltpu.HBM) for x in operands])


def score_kernel(grads_ref, fisher_ref, query_ref, scores_ref, grads, turned, solved):
    slots, examples, size = grads_ref.shape
    rows = slots * examples
    cut = -(-size // 2 // MXU) * MXU
    grads[...] = grads_ref[...].reshape(rows, size)
    turned[...] = query_ref[0].T
    total = jnp.dot(grads[:, :cut], fisher_ref[0, :cut], preferred_element_type=jnp.float32) + jnp.dot(
        grads[:, cut:], fisher_ref[0, cut:], preferred_element_type=jnp.float32
    )
    main = total.astype(jnp.bfloat16)
    rest = (total - main.astype(jnp.float32)).astype(jnp.bfloat16)
    solved[...] = jnp.concatenate([main, rest], axis=0)
    both = jnp.dot(solved[...], turned[...], preferred_element_type=jnp.float32)
    scores_ref[...] = (both[:rows] + both[rows:]).astype(scores_ref.dtype).reshape(scores_ref.shape)


def module_scores(grads, fisher, query):
    slots, examples, size = grads.shape
    rows, queries = slots * examples, query.shape[1]
    return pl.pallas_call(
        score_kernel,
        out_shape=jax.ShapeDtypeStruct((slots, examples, queries), jnp.bfloat16),
        in_specs=[pl.BlockSpec(memory_space=pltpu.VMEM)] * 3,
        out_specs=pl.BlockSpec(memory_space=pltpu.VMEM),
        scratch_shapes=[
            pltpu.VMEM((rows, size), jnp.bfloat16),
            pltpu.VMEM((size, queries), jnp.bfloat16),
            pltpu.VMEM((2 * rows, size), jnp.bfloat16),
        ],
        compiler_params=pltpu.CompilerParams(vmem_limit_bytes=24 << 20),
        cost_estimate=pl.CostEstimate(
            flops=2 * rows * (fisher.size + 2 * query.size),
            bytes_accessed=2 * (fisher.size + query.size),
            transcendentals=0,
        ),
    )(grads, fisher, query)


def local(inputs_proj, outputs_proj, lengths, owner, fisher_inv, query_grads):
    routed = form_grads(inputs_proj, outputs_proj, lengths, owner)
    received = lax.all_to_all(routed, "mod", split_axis=0, concat_axis=0, tiled=True)
    partial = module_scores(received, fisher_inv, query_grads)
    spread = lax.all_to_all(partial, "mod", split_axis=0, concat_axis=0, tiled=True)
    return jnp.sum(spread.astype(jnp.float32), axis=0)


def solution(mesh):
    return jax.shard_map(
        local,
        mesh=mesh,
        in_specs=(
            P(("grp", "mod"), None, None),
            P(("grp", "mod"), None, None),
            P(("grp", "mod")),
            P(),
            P("mod", None, None),
            P("mod", None, None),
        ),
        out_specs=P(("grp", "mod"), None),
        check_vma=False,
    )
```

```python
import functools

import jax
import jax.numpy as jnp
from jax import lax
from jax.experimental import pallas as pl
from jax.experimental.pallas import tpu as pltpu
from jax.sharding import PartitionSpec as P

OUT_RANK = 40
IN_RANK = 48
SEQ_LEN = 32
LANES = 128
HALF = LANES // 2
MXU = 256
HALF_OUT = OUT_RANK // 2
BLOCK_IN = 16
PITCH = SEQ_LEN + 4
LONG = pl.CostEstimate(flops=20_000_000_000, bytes_accessed=30_000_000, transcendentals=0)


def form_kernel(
    examples, owner_hbm, lengths_hbm, in_hbm, out_hbm, grads_ref,
    owner_ref, lengths_ref, in_ref, out_ref, in_t, out_t, formed, arrived,
):
    modules = HALF // examples
    here = pl.ds(pl.program_id(0) * modules, modules)
    pairs = (
        (in_hbm.at[:, here], in_ref),
        (out_hbm.at[:, here], out_ref),
        (lengths_hbm, lengths_ref),
        (owner_hbm, owner_ref),
    )
    copies = [pltpu.make_async_copy(there, mine, arrived.at[k]) for k, (there, mine) in enumerate(pairs)]
    for copy in copies:
        copy.start()
    for copy in copies:
        copy.wait()

    half_cols = HALF_OUT * SEQ_LEN
    inputs = in_ref[...].reshape(HALF, in_ref.shape[2])
    outputs = out_ref[...].reshape(HALF, out_ref.shape[2])
    turned_in = jnp.concatenate([inputs, inputs], axis=0).T.astype(jnp.float32)
    for i in range(IN_RANK):
        in_t[pl.ds(i * PITCH, SEQ_LEN), :] = turned_in[i * SEQ_LEN : (i + 1) * SEQ_LEN]
    turned = jnp.concatenate([outputs[:, :half_cols], outputs[:, half_cols:]], axis=0).T.astype(jnp.float32)

    example = lax.broadcasted_iota(jnp.int32, (half_cols, LANES), 1) % HALF // modules
    live = jnp.zeros((half_cols, LANES), jnp.int32)
    for e in range(examples):
        live = jnp.where(example == e, lengths_ref[e], live)
    slot_t = lax.broadcasted_iota(jnp.int32, (half_cols, LANES), 0) % SEQ_LEN
    out_t[...] = jnp.where(slot_t < live, turned, 0.0)

    @pl.loop(0, IN_RANK // BLOCK_IN)
    def _(block):
        first = block * (BLOCK_IN * PITCH)
        sums = [jnp.zeros((BLOCK_IN, LANES), jnp.float32) for _ in range(HALF_OUT)]
        for t in range(SEQ_LEN):
            features = in_t[pl.ds(first + t, BLOCK_IN, stride=PITCH), :]
            for o in range(HALF_OUT):
                sums[o] = sums[o] + features * out_t[pl.ds(o * SEQ_LEN + t, 1), :]
        for o in range(HALF_OUT):
            start = pl.multiple_of(o * IN_RANK + block * BLOCK_IN, BLOCK_IN)
            formed[pl.ds(start, BLOCK_IN), :] = sums[o].astype(jnp.bfloat16)

    row = lax.broadcasted_iota(jnp.int32, (HALF, HALF), 0)
    lane = lax.broadcasted_iota(jnp.int32, (HALF, HALF), 1)
    pick = jnp.where(lane == row % examples * modules + row // examples, 1.0, 0.0).astype(jnp.bfloat16)
    blank = jnp.zeros_like(pick)
    low = jnp.concatenate([pick, blank], axis=1)
    high = jnp.concatenate([blank, pick], axis=1)

    def take(side, first, last):
        return lax.dot_general(side, formed[first:last], (((1,), (1,)), ((), ())), preferred_element_type=jnp.float32)

    half = HALF_OUT * IN_RANK
    whole = half // LANES * LANES
    parts = [take(low, 0, whole)]
    if whole < half:
        edge = jnp.concatenate([formed[whole:half], formed[: whole + LANES - half]], axis=0)
        upper = lax.broadcasted_iota(jnp.int32, (HALF, LANES), 1) >= half - whole
        over_lanes = (((1,), (1,)), ((), ()))
        parts.append(
            jnp.where(
                upper,
                lax.dot_general(high, edge, over_lanes, preferred_element_type=jnp.float32),
                lax.dot_general(low, edge, over_lanes, preferred_element_type=jnp.float32),
            )
        )
        parts.append(take(high, whole + LANES - half, half))
    else:
        parts.append(take(high, 0, half))
    grads = jnp.concatenate(parts, axis=1).astype(jnp.bfloat16)
    for m in range(modules):
        slot = owner_ref[pl.program_id(0) * modules + m]
        grads_ref[slot] = grads[m * examples : (m + 1) * examples]


def form_grads(inputs_proj, outputs_proj, lengths, owner):
    examples, modules, in_cols = inputs_proj.shape
    out_cols = outputs_proj.shape[2]
    step = HALF // examples
    shape = (modules, examples, OUT_RANK * IN_RANK)
    operands = (owner, lengths, inputs_proj, outputs_proj)
    return pl.pallas_call(
        functools.partial(form_kernel, examples),
        out_shape=jax.ShapeDtypeStruct(shape, jnp.bfloat16),
        grid=(modules // step,),
        in_specs=[pl.BlockSpec(memory_space=pltpu.HBM)] * 4,
        out_specs=pl.BlockSpec(shape, lambda i: (0, 0, 0)),
        scratch_shapes=[
            pltpu.SMEM((modules,), jnp.int32),
            pltpu.SMEM((examples,), jnp.int32),
            pltpu.VMEM((examples, step, in_cols), jnp.bfloat16),
            pltpu.VMEM((examples, step, out_cols), jnp.bfloat16),
            pltpu.VMEM((IN_RANK * PITCH, LANES), jnp.float32),
            pltpu.VMEM((HALF_OUT * SEQ_LEN, LANES), jnp.float32),
            pltpu.VMEM((HALF_OUT * IN_RANK, LANES), jnp.bfloat16),
            pltpu.SemaphoreType.DMA((4,)),
        ],
        compiler_params=pltpu.CompilerParams(vmem_limit_bytes=24 << 20),
        cost_estimate=LONG,
    )(*[pltpu.with_memory_space_constraint(x, pltpu.HBM) for x in operands])


def score_kernel(places, grads_ref, fisher_ref, query_ref, scores_ref, grads, turned, solved):
    slots, examples, size = grads_ref.shape
    rows = slots * examples
    cut = -(-size // 2 // MXU) * MXU
    grads[...] = grads_ref[...].reshape(rows, size)
    turned[...] = query_ref[0].T
    total = jnp.dot(grads[:, :cut], fisher_ref[0, :cut], preferred_element_type=jnp.float32) + jnp.dot(
        grads[:, cut:], fisher_ref[0, cut:], preferred_element_type=jnp.float32
    )
    main = total.astype(jnp.bfloat16)
    rest = (total - main.astype(jnp.float32)).astype(jnp.bfloat16)
    solved[...] = jnp.concatenate([main, rest], axis=0)
    both = jnp.dot(solved[...], turned[...], preferred_element_type=jnp.float32)
    scores = (both[:rows] + both[rows:]).astype(scores_ref.dtype)
    for source, place in enumerate(places):
        scores_ref[place] = scores[source * examples : (source + 1) * examples]


def module_scores(grads, fisher, query, order):
    slots, examples, size = grads.shape
    rows, queries = slots * examples, query.shape[1]
    places = [order.index(source) for source in range(slots)]
    return pl.pallas_call(
        functools.partial(score_kernel, places),
        out_shape=jax.ShapeDtypeStruct((slots, examples, queries), jnp.bfloat16),
        in_specs=[pl.BlockSpec(memory_space=pltpu.VMEM)] * 3,
        out_specs=pl.BlockSpec(memory_space=pltpu.VMEM),
        scratch_shapes=[
            pltpu.VMEM((rows, size), jnp.bfloat16),
            pltpu.VMEM((size, queries), jnp.bfloat16),
            pltpu.VMEM((2 * rows, size), jnp.bfloat16),
        ],
        compiler_params=pltpu.CompilerParams(vmem_limit_bytes=24 << 20),
        cost_estimate=pl.CostEstimate(
            flops=2 * rows * (fisher.size + 2 * query.size),
            bytes_accessed=2 * (fisher.size + query.size),
            transcendentals=0,
        ),
    )(grads, fisher, query)


def local(inputs_proj, outputs_proj, lengths, owner, fisher_inv, query_grads):
    routed = form_grads(inputs_proj, outputs_proj, lengths, owner)
    received = lax.all_to_all(routed, "mod", split_axis=0, concat_axis=0, tiled=True)
    count = received.shape[0]
    far = 2 ** ((count.bit_length() - 1) // 2)
    near = count // far
    order = [far_index * near + near_index for near_index in range(near) for far_index in range(far)]
    partial = module_scores(received, fisher_inv, query_grads, order)
    spread = lax.all_to_all(partial, "mod", split_axis=0, concat_axis=0, axis_index_groups=[order], tiled=True)
    return jnp.sum(spread.astype(jnp.float32), axis=0)


def solution(mesh):
    return jax.shard_map(
        local,
        mesh=mesh,
        in_specs=(
            P(("grp", "mod"), None, None),
            P(("grp", "mod"), None, None),
            P(("grp", "mod")),
            P(),
            P("mod", None, None),
            P("mod", None, None),
        ),
        out_specs=P(("grp", "mod"), None),
        check_vma=False,
    )
```

```python
import functools

import jax
import jax.numpy as jnp
from jax import lax
from jax.experimental import pallas as pl
from jax.experimental.pallas import tpu as pltpu
from jax.sharding import PartitionSpec as P

OUT_RANK = 40
IN_RANK = 48
SEQ_LEN = 32
LANES = 128
HALF = LANES // 2
MXU = 256
HALF_OUT = OUT_RANK // 2
BLOCK_IN = 16
PITCH = SEQ_LEN + 4
LONG = pl.CostEstimate(flops=20_000_000_000, bytes_accessed=30_000_000, transcendentals=0)


def first_listed(count):
    return 3 * count // 4 - 1


def listed(count):
    order = list(range(count))[::-1]
    first = order.index(first_listed(count))
    order[0], order[first] = order[first], order[0]
    return order


def place_of(slot, count):
    first, last = first_listed(count), count - 1
    return jnp.where(slot == first, 0, jnp.where(slot == last, last - first, last - slot))


def form_kernel(
    examples, owner_hbm, lengths_hbm, in_hbm, out_hbm, grads_ref,
    owner_ref, lengths_ref, in_ref, out_ref, in_t, out_t, formed, arrived,
):
    modules = HALF // examples
    here = pl.ds(pl.program_id(0) * modules, modules)
    pairs = (
        (in_hbm.at[:, here], in_ref),
        (out_hbm.at[:, here], out_ref),
        (lengths_hbm, lengths_ref),
        (owner_hbm, owner_ref),
    )
    copies = [pltpu.make_async_copy(there, mine, arrived.at[k]) for k, (there, mine) in enumerate(pairs)]
    for copy in copies:
        copy.start()
    for copy in copies:
        copy.wait()

    half_cols = HALF_OUT * SEQ_LEN
    inputs = in_ref[...].reshape(HALF, in_ref.shape[2])
    outputs = out_ref[...].reshape(HALF, out_ref.shape[2])
    turned_in = jnp.concatenate([inputs, inputs], axis=0).T.astype(jnp.float32)
    for i in range(IN_RANK):
        in_t[pl.ds(i * PITCH, SEQ_LEN), :] = turned_in[i * SEQ_LEN : (i + 1) * SEQ_LEN]
    turned = jnp.concatenate([outputs[:, :half_cols], outputs[:, half_cols:]], axis=0).T.astype(jnp.float32)

    example = lax.broadcasted_iota(jnp.int32, (half_cols, LANES), 1) % HALF // modules
    live = jnp.zeros((half_cols, LANES), jnp.int32)
    for e in range(examples):
        live = jnp.where(example == e, lengths_ref[e], live)
    slot_t = lax.broadcasted_iota(jnp.int32, (half_cols, LANES), 0) % SEQ_LEN
    out_t[...] = jnp.where(slot_t < live, turned, 0.0)

    @pl.loop(0, IN_RANK // BLOCK_IN)
    def _(block):
        first = block * (BLOCK_IN * PITCH)
        sums = [jnp.zeros((BLOCK_IN, LANES), jnp.float32) for _ in range(HALF_OUT)]
        for t in range(SEQ_LEN):
            features = in_t[pl.ds(first + t, BLOCK_IN, stride=PITCH), :]
            for o in range(HALF_OUT):
                sums[o] = sums[o] + features * out_t[pl.ds(o * SEQ_LEN + t, 1), :]
        for o in range(HALF_OUT):
            start = pl.multiple_of(o * IN_RANK + block * BLOCK_IN, BLOCK_IN)
            formed[pl.ds(start, BLOCK_IN), :] = sums[o].astype(jnp.bfloat16)

    row = lax.broadcasted_iota(jnp.int32, (HALF, HALF), 0)
    lane = lax.broadcasted_iota(jnp.int32, (HALF, HALF), 1)
    pick = jnp.where(lane == row % examples * modules + row // examples, 1.0, 0.0).astype(jnp.bfloat16)
    blank = jnp.zeros_like(pick)
    low = jnp.concatenate([pick, blank], axis=1)
    high = jnp.concatenate([blank, pick], axis=1)

    def take(side, first, last):
        return lax.dot_general(side, formed[first:last], (((1,), (1,)), ((), ())), preferred_element_type=jnp.float32)

    half = HALF_OUT * IN_RANK
    whole = half // LANES * LANES
    parts = [take(low, 0, whole)]
    if whole < half:
        edge = jnp.concatenate([formed[whole:half], formed[: whole + LANES - half]], axis=0)
        upper = lax.broadcasted_iota(jnp.int32, (HALF, LANES), 1) >= half - whole
        over_lanes = (((1,), (1,)), ((), ()))
        parts.append(
            jnp.where(
                upper,
                lax.dot_general(high, edge, over_lanes, preferred_element_type=jnp.float32),
                lax.dot_general(low, edge, over_lanes, preferred_element_type=jnp.float32),
            )
        )
        parts.append(take(high, whole + LANES - half, half))
    else:
        parts.append(take(high, 0, half))
    grads = jnp.concatenate(parts, axis=1).astype(jnp.bfloat16)
    for m in range(modules):
        slot = owner_ref[pl.program_id(0) * modules + m]
        grads_ref[place_of(slot, grads_ref.shape[0])] = grads[m * examples : (m + 1) * examples]


def form_grads(inputs_proj, outputs_proj, lengths, owner):
    examples, modules, in_cols = inputs_proj.shape
    out_cols = outputs_proj.shape[2]
    step = HALF // examples
    shape = (modules, examples, OUT_RANK * IN_RANK)
    operands = (owner, lengths, inputs_proj, outputs_proj)
    return pl.pallas_call(
        functools.partial(form_kernel, examples),
        out_shape=jax.ShapeDtypeStruct(shape, jnp.bfloat16),
        grid=(modules // step,),
        in_specs=[pl.BlockSpec(memory_space=pltpu.HBM)] * 4,
        out_specs=pl.BlockSpec(shape, lambda i: (0, 0, 0)),
        scratch_shapes=[
            pltpu.SMEM((modules,), jnp.int32),
            pltpu.SMEM((examples,), jnp.int32),
            pltpu.VMEM((examples, step, in_cols), jnp.bfloat16),
            pltpu.VMEM((examples, step, out_cols), jnp.bfloat16),
            pltpu.VMEM((IN_RANK * PITCH, LANES), jnp.float32),
            pltpu.VMEM((HALF_OUT * SEQ_LEN, LANES), jnp.float32),
            pltpu.VMEM((HALF_OUT * IN_RANK, LANES), jnp.bfloat16),
            pltpu.SemaphoreType.DMA((4,)),
        ],
        compiler_params=pltpu.CompilerParams(vmem_limit_bytes=24 << 20),
        cost_estimate=LONG,
    )(*[pltpu.with_memory_space_constraint(x, pltpu.HBM) for x in operands])


def score_kernel(grads_ref, fisher_ref, query_ref, scores_ref, grads, turned, solved):
    slots, examples, size = grads_ref.shape
    rows = slots * examples
    cut = -(-size // 2 // MXU) * MXU
    grads[...] = grads_ref[...].reshape(rows, size)
    turned[...] = query_ref[0].T
    total = jnp.dot(grads[:, :cut], fisher_ref[0, :cut], preferred_element_type=jnp.float32) + jnp.dot(
        grads[:, cut:], fisher_ref[0, cut:], preferred_element_type=jnp.float32
    )
    main = total.astype(jnp.bfloat16)
    rest = (total - main.astype(jnp.float32)).astype(jnp.bfloat16)
    solved[...] = jnp.concatenate([main, rest], axis=0)
    both = jnp.dot(solved[...], turned[...], preferred_element_type=jnp.float32)
    scores_ref[...] = (both[:rows] + both[rows:]).astype(scores_ref.dtype).reshape(scores_ref.shape)


def module_scores(grads, fisher, query):
    slots, examples, size = grads.shape
    rows, queries = slots * examples, query.shape[1]
    return pl.pallas_call(
        score_kernel,
        out_shape=jax.ShapeDtypeStruct((slots, examples, queries), jnp.bfloat16),
        in_specs=[pl.BlockSpec(memory_space=pltpu.VMEM)] * 3,
        out_specs=pl.BlockSpec(memory_space=pltpu.VMEM),
        scratch_shapes=[
            pltpu.VMEM((rows, size), jnp.bfloat16),
            pltpu.VMEM((size, queries), jnp.bfloat16),
            pltpu.VMEM((2 * rows, size), jnp.bfloat16),
        ],
        compiler_params=pltpu.CompilerParams(vmem_limit_bytes=24 << 20),
        cost_estimate=pl.CostEstimate(
            flops=2 * rows * (fisher.size + 2 * query.size),
            bytes_accessed=2 * (fisher.size + query.size),
            transcendentals=0,
        ),
    )(grads, fisher, query)


def local(inputs_proj, outputs_proj, lengths, owner, fisher_inv, query_grads):
    groups = [listed(owner.shape[0])]
    routed = form_grads(inputs_proj, outputs_proj, lengths, owner)
    received = lax.all_to_all(routed, "mod", split_axis=0, concat_axis=0, axis_index_groups=groups, tiled=True)
    partial = module_scores(received, fisher_inv, query_grads)
    spread = lax.all_to_all(partial, "mod", split_axis=0, concat_axis=0, axis_index_groups=groups, tiled=True)
    return jnp.sum(spread.astype(jnp.float32), axis=0)


def solution(mesh):
    return jax.shard_map(
        local,
        mesh=mesh,
        in_specs=(
            P(("grp", "mod"), None, None),
            P(("grp", "mod"), None, None),
            P(("grp", "mod")),
            P(),
            P("mod", None, None),
            P("mod", None, None),
        ),
        out_specs=P(("grp", "mod"), None),
        check_vma=False,
    )
```

```python
import functools

import jax
import jax.numpy as jnp
from jax import lax
from jax.experimental import pallas as pl
from jax.experimental.pallas import tpu as pltpu
from jax.sharding import PartitionSpec as P

OUT_RANK = 40
IN_RANK = 48
SEQ_LEN = 32
LANES = 128
HALF = LANES // 2
MXU = 256
HALF_OUT = OUT_RANK // 2
BLOCK_IN = 16
PITCH = SEQ_LEN + 4
LONG = pl.CostEstimate(flops=20_000_000_000, bytes_accessed=30_000_000, transcendentals=0)


def first_listed(count):
    return 3 * count // 4 - 1


def listed(count):
    order = list(range(count))[::-1]
    first = order.index(first_listed(count))
    order[0], order[first] = order[first], order[0]
    return order


def listed_by_distance(count):
    first = first_listed(count)
    near = count // 2 ** ((count.bit_length() - 1) // 2)

    def distance(device):
        apart = abs(device // near - first // near) + abs(device % near // 2 - first % near // 2)
        return (apart, device % 2 != first % 2)

    others = sorted((device for device in range(count) if device != first), key=distance, reverse=True)
    return [first, *others]


def place_of(slot, count):
    first, last = first_listed(count), count - 1
    return jnp.where(slot == first, 0, jnp.where(slot == last, last - first, last - slot))


def form_kernel(
    examples, owner_hbm, lengths_hbm, in_hbm, out_hbm, grads_ref,
    owner_ref, lengths_ref, in_ref, out_ref, in_t, out_t, formed, arrived,
):
    modules = HALF // examples
    here = pl.ds(pl.program_id(0) * modules, modules)
    pairs = (
        (in_hbm.at[:, here], in_ref),
        (out_hbm.at[:, here], out_ref),
        (lengths_hbm, lengths_ref),
        (owner_hbm, owner_ref),
    )
    copies = [pltpu.make_async_copy(there, mine, arrived.at[k]) for k, (there, mine) in enumerate(pairs)]
    for copy in copies:
        copy.start()
    for copy in copies:
        copy.wait()

    half_cols = HALF_OUT * SEQ_LEN
    inputs = in_ref[...].reshape(HALF, in_ref.shape[2])
    outputs = out_ref[...].reshape(HALF, out_ref.shape[2])
    turned_in = jnp.concatenate([inputs, inputs], axis=0).T.astype(jnp.float32)
    for i in range(IN_RANK):
        in_t[pl.ds(i * PITCH, SEQ_LEN), :] = turned_in[i * SEQ_LEN : (i + 1) * SEQ_LEN]
    turned = jnp.concatenate([outputs[:, :half_cols], outputs[:, half_cols:]], axis=0).T.astype(jnp.float32)

    example = lax.broadcasted_iota(jnp.int32, (half_cols, LANES), 1) % HALF // modules
    live = jnp.zeros((half_cols, LANES), jnp.int32)
    for e in range(examples):
        live = jnp.where(example == e, lengths_ref[e], live)
    slot_t = lax.broadcasted_iota(jnp.int32, (half_cols, LANES), 0) % SEQ_LEN
    out_t[...] = jnp.where(slot_t < live, turned, 0.0)

    @pl.loop(0, IN_RANK // BLOCK_IN)
    def _(block):
        first = block * (BLOCK_IN * PITCH)
        sums = [jnp.zeros((BLOCK_IN, LANES), jnp.float32) for _ in range(HALF_OUT)]
        for t in range(SEQ_LEN):
            features = in_t[pl.ds(first + t, BLOCK_IN, stride=PITCH), :]
            for o in range(HALF_OUT):
                sums[o] = sums[o] + features * out_t[pl.ds(o * SEQ_LEN + t, 1), :]
        for o in range(HALF_OUT):
            start = pl.multiple_of(o * IN_RANK + block * BLOCK_IN, BLOCK_IN)
            formed[pl.ds(start, BLOCK_IN), :] = sums[o].astype(jnp.bfloat16)

    row = lax.broadcasted_iota(jnp.int32, (HALF, HALF), 0)
    lane = lax.broadcasted_iota(jnp.int32, (HALF, HALF), 1)
    pick = jnp.where(lane == row % examples * modules + row // examples, 1.0, 0.0).astype(jnp.bfloat16)
    blank = jnp.zeros_like(pick)
    low = jnp.concatenate([pick, blank], axis=1)
    high = jnp.concatenate([blank, pick], axis=1)

    def take(side, first, last):
        return lax.dot_general(side, formed[first:last], (((1,), (1,)), ((), ())), preferred_element_type=jnp.float32)

    half = HALF_OUT * IN_RANK
    whole = half // LANES * LANES
    parts = [take(low, 0, whole)]
    if whole < half:
        edge = jnp.concatenate([formed[whole:half], formed[: whole + LANES - half]], axis=0)
        upper = lax.broadcasted_iota(jnp.int32, (HALF, LANES), 1) >= half - whole
        over_lanes = (((1,), (1,)), ((), ()))
        parts.append(
            jnp.where(
                upper,
                lax.dot_general(high, edge, over_lanes, preferred_element_type=jnp.float32),
                lax.dot_general(low, edge, over_lanes, preferred_element_type=jnp.float32),
            )
        )
        parts.append(take(high, whole + LANES - half, half))
    else:
        parts.append(take(high, 0, half))
    grads = jnp.concatenate(parts, axis=1).astype(jnp.bfloat16)
    for m in range(modules):
        slot = owner_ref[pl.program_id(0) * modules + m]
        grads_ref[place_of(slot, grads_ref.shape[0])] = grads[m * examples : (m + 1) * examples]


def form_grads(inputs_proj, outputs_proj, lengths, owner):
    examples, modules, in_cols = inputs_proj.shape
    out_cols = outputs_proj.shape[2]
    step = HALF // examples
    shape = (modules, examples, OUT_RANK * IN_RANK)
    operands = (owner, lengths, inputs_proj, outputs_proj)
    return pl.pallas_call(
        functools.partial(form_kernel, examples),
        out_shape=jax.ShapeDtypeStruct(shape, jnp.bfloat16),
        grid=(modules // step,),
        in_specs=[pl.BlockSpec(memory_space=pltpu.HBM)] * 4,
        out_specs=pl.BlockSpec(shape, lambda i: (0, 0, 0)),
        scratch_shapes=[
            pltpu.SMEM((modules,), jnp.int32),
            pltpu.SMEM((examples,), jnp.int32),
            pltpu.VMEM((examples, step, in_cols), jnp.bfloat16),
            pltpu.VMEM((examples, step, out_cols), jnp.bfloat16),
            pltpu.VMEM((IN_RANK * PITCH, LANES), jnp.float32),
            pltpu.VMEM((HALF_OUT * SEQ_LEN, LANES), jnp.float32),
            pltpu.VMEM((HALF_OUT * IN_RANK, LANES), jnp.bfloat16),
            pltpu.SemaphoreType.DMA((4,)),
        ],
        compiler_params=pltpu.CompilerParams(vmem_limit_bytes=24 << 20),
        cost_estimate=LONG,
    )(*[pltpu.with_memory_space_constraint(x, pltpu.HBM) for x in operands])


def score_kernel(places, grads_ref, fisher_ref, query_ref, scores_ref, grads, turned, solved):
    slots, examples, size = grads_ref.shape
    rows = slots * examples
    cut = -(-size // 2 // MXU) * MXU
    grads[...] = grads_ref[...].reshape(rows, size)
    turned[...] = query_ref[0].T
    total = jnp.dot(grads[:, :cut], fisher_ref[0, :cut], preferred_element_type=jnp.float32) + jnp.dot(
        grads[:, cut:], fisher_ref[0, cut:], preferred_element_type=jnp.float32
    )
    main = total.astype(jnp.bfloat16)
    rest = (total - main.astype(jnp.float32)).astype(jnp.bfloat16)
    solved[...] = jnp.concatenate([main, rest], axis=0)
    both = jnp.dot(solved[...], turned[...], preferred_element_type=jnp.float32)
    scores = (both[:rows] + both[rows:]).astype(scores_ref.dtype)
    for block, place in enumerate(places):
        scores_ref[place] = scores[block * examples : (block + 1) * examples]


def module_scores(grads, fisher, query, places):
    slots, examples, size = grads.shape
    rows, queries = slots * examples, query.shape[1]
    return pl.pallas_call(
        functools.partial(score_kernel, places),
        out_shape=jax.ShapeDtypeStruct((slots, examples, queries), jnp.bfloat16),
        in_specs=[pl.BlockSpec(memory_space=pltpu.VMEM)] * 3,
        out_specs=pl.BlockSpec(memory_space=pltpu.VMEM),
        scratch_shapes=[
            pltpu.VMEM((rows, size), jnp.bfloat16),
            pltpu.VMEM((size, queries), jnp.bfloat16),
            pltpu.VMEM((2 * rows, size), jnp.bfloat16),
        ],
        compiler_params=pltpu.CompilerParams(vmem_limit_bytes=24 << 20),
        cost_estimate=pl.CostEstimate(
            flops=2 * rows * (fisher.size + 2 * query.size),
            bytes_accessed=2 * (fisher.size + query.size),
            transcendentals=0,
        ),
    )(grads, fisher, query)


def local(inputs_proj, outputs_proj, lengths, owner, fisher_inv, query_grads):
    count = owner.shape[0]
    out, back = listed(count), listed_by_distance(count)
    routed = form_grads(inputs_proj, outputs_proj, lengths, owner)
    received = lax.all_to_all(routed, "mod", split_axis=0, concat_axis=0, axis_index_groups=[out], tiled=True)
    partial = module_scores(received, fisher_inv, query_grads, [back.index(device) for device in out])
    spread = lax.all_to_all(partial, "mod", split_axis=0, concat_axis=0, axis_index_groups=[back], tiled=True)
    return jnp.sum(spread.astype(jnp.float32), axis=0)


def solution(mesh):
    return jax.shard_map(
        local,
        mesh=mesh,
        in_specs=(
            P(("grp", "mod"), None, None),
            P(("grp", "mod"), None, None),
            P(("grp", "mod")),
            P(),
            P("mod", None, None),
            P("mod", None, None),
        ),
        out_specs=P(("grp", "mod"), None),
        check_vma=False,
    )
```

```python
import functools

import jax
import jax.numpy as jnp
from jax import lax
from jax.experimental import pallas as pl
from jax.experimental.pallas import tpu as pltpu
from jax.sharding import PartitionSpec as P

OUT_RANK = 40
IN_RANK = 48
SEQ_LEN = 32
LANES = 128
HALF = LANES // 2
MXU = 256
HALF_OUT = OUT_RANK // 2
BLOCK_IN = 16
PITCH = SEQ_LEN + 4
LONG = pl.CostEstimate(flops=20_000_000_000, bytes_accessed=30_000_000, transcendentals=0)


def first_listed(count):
    return 3 * count // 4 - 1


def listed(count):
    first = first_listed(count)
    return [(first - place) % count for place in range(count)]


def listed_by_distance(count):
    first = first_listed(count)
    near = count // 2 ** ((count.bit_length() - 1) // 2)

    def distance(device):
        apart = abs(device // near - first // near) + abs(device % near // 2 - first % near // 2)
        return (apart, device % 2 != first % 2)

    others = sorted((device for device in range(count) if device != first), key=distance, reverse=True)
    return [first, *others]


def place_of(slot, count):
    behind = first_listed(count) - slot
    return jnp.where(behind < 0, behind + count, behind)


def form_kernel(
    examples, owner_hbm, lengths_hbm, in_hbm, out_hbm, grads_ref,
    owner_ref, lengths_ref, in_ref, out_ref, in_t, out_t, formed, arrived,
):
    modules = HALF // examples
    here = pl.ds(pl.program_id(0) * modules, modules)
    pairs = (
        (in_hbm.at[:, here], in_ref),
        (out_hbm.at[:, here], out_ref),
        (lengths_hbm, lengths_ref),
        (owner_hbm, owner_ref),
    )
    copies = [pltpu.make_async_copy(there, mine, arrived.at[k]) for k, (there, mine) in enumerate(pairs)]
    for copy in copies:
        copy.start()
    for copy in copies:
        copy.wait()

    half_cols = HALF_OUT * SEQ_LEN
    inputs = in_ref[...].reshape(HALF, in_ref.shape[2])
    outputs = out_ref[...].reshape(HALF, out_ref.shape[2])
    turned_in = jnp.concatenate([inputs, inputs], axis=0).T.astype(jnp.float32)
    for i in range(IN_RANK):
        in_t[pl.ds(i * PITCH, SEQ_LEN), :] = turned_in[i * SEQ_LEN : (i + 1) * SEQ_LEN]
    turned = jnp.concatenate([outputs[:, :half_cols], outputs[:, half_cols:]], axis=0).T.astype(jnp.float32)

    example = lax.broadcasted_iota(jnp.int32, (half_cols, LANES), 1) % HALF // modules
    live = jnp.zeros((half_cols, LANES), jnp.int32)
    for e in range(examples):
        live = jnp.where(example == e, lengths_ref[e], live)
    slot_t = lax.broadcasted_iota(jnp.int32, (half_cols, LANES), 0) % SEQ_LEN
    out_t[...] = jnp.where(slot_t < live, turned, 0.0)

    @pl.loop(0, IN_RANK // BLOCK_IN)
    def _(block):
        first = block * (BLOCK_IN * PITCH)
        sums = [jnp.zeros((BLOCK_IN, LANES), jnp.float32) for _ in range(HALF_OUT)]
        for t in range(SEQ_LEN):
            features = in_t[pl.ds(first + t, BLOCK_IN, stride=PITCH), :]
            for o in range(HALF_OUT):
                sums[o] = sums[o] + features * out_t[pl.ds(o * SEQ_LEN + t, 1), :]
        for o in range(HALF_OUT):
            start = pl.multiple_of(o * IN_RANK + block * BLOCK_IN, BLOCK_IN)
            formed[pl.ds(start, BLOCK_IN), :] = sums[o].astype(jnp.bfloat16)

    row = lax.broadcasted_iota(jnp.int32, (HALF, HALF), 0)
    lane = lax.broadcasted_iota(jnp.int32, (HALF, HALF), 1)
    pick = jnp.where(lane == row % examples * modules + row // examples, 1.0, 0.0).astype(jnp.bfloat16)
    blank = jnp.zeros_like(pick)
    low = jnp.concatenate([pick, blank], axis=1)
    high = jnp.concatenate([blank, pick], axis=1)

    def take(side, first, last):
        return lax.dot_general(side, formed[first:last], (((1,), (1,)), ((), ())), preferred_element_type=jnp.float32)

    half = HALF_OUT * IN_RANK
    whole = half // LANES * LANES
    parts = [take(low, 0, whole)]
    if whole < half:
        edge = jnp.concatenate([formed[whole:half], formed[: whole + LANES - half]], axis=0)
        upper = lax.broadcasted_iota(jnp.int32, (HALF, LANES), 1) >= half - whole
        over_lanes = (((1,), (1,)), ((), ()))
        parts.append(
            jnp.where(
                upper,
                lax.dot_general(high, edge, over_lanes, preferred_element_type=jnp.float32),
                lax.dot_general(low, edge, over_lanes, preferred_element_type=jnp.float32),
            )
        )
        parts.append(take(high, whole + LANES - half, half))
    else:
        parts.append(take(high, 0, half))
    grads = jnp.concatenate(parts, axis=1).astype(jnp.bfloat16)
    for m in range(modules):
        slot = owner_ref[pl.program_id(0) * modules + m]
        grads_ref[place_of(slot, grads_ref.shape[0])] = grads[m * examples : (m + 1) * examples]


def form_grads(inputs_proj, outputs_proj, lengths, owner):
    examples, modules, in_cols = inputs_proj.shape
    out_cols = outputs_proj.shape[2]
    step = HALF // examples
    shape = (modules, examples, OUT_RANK * IN_RANK)
    operands = (owner, lengths, inputs_proj, outputs_proj)
    return pl.pallas_call(
        functools.partial(form_kernel, examples),
        out_shape=jax.ShapeDtypeStruct(shape, jnp.bfloat16),
        grid=(modules // step,),
        in_specs=[pl.BlockSpec(memory_space=pltpu.HBM)] * 4,
        out_specs=pl.BlockSpec(shape, lambda i: (0, 0, 0)),
        scratch_shapes=[
            pltpu.SMEM((modules,), jnp.int32),
            pltpu.SMEM((examples,), jnp.int32),
            pltpu.VMEM((examples, step, in_cols), jnp.bfloat16),
            pltpu.VMEM((examples, step, out_cols), jnp.bfloat16),
            pltpu.VMEM((IN_RANK * PITCH, LANES), jnp.float32),
            pltpu.VMEM((HALF_OUT * SEQ_LEN, LANES), jnp.float32),
            pltpu.VMEM((HALF_OUT * IN_RANK, LANES), jnp.bfloat16),
            pltpu.SemaphoreType.DMA((4,)),
        ],
        compiler_params=pltpu.CompilerParams(vmem_limit_bytes=24 << 20),
        cost_estimate=LONG,
    )(*[pltpu.with_memory_space_constraint(x, pltpu.HBM) for x in operands])


def score_kernel(places, grads_ref, fisher_ref, query_ref, scores_ref, grads, turned, solved):
    slots, examples, size = grads_ref.shape
    rows = slots * examples
    cut = -(-size // 2 // MXU) * MXU
    grads[...] = grads_ref[...].reshape(rows, size)
    turned[...] = query_ref[0].T
    total = jnp.dot(grads[:, :cut], fisher_ref[0, :cut], preferred_element_type=jnp.float32) + jnp.dot(
        grads[:, cut:], fisher_ref[0, cut:], preferred_element_type=jnp.float32
    )
    main = total.astype(jnp.bfloat16)
    rest = (total - main.astype(jnp.float32)).astype(jnp.bfloat16)
    solved[...] = jnp.concatenate([main, rest], axis=0)
    both = jnp.dot(solved[...], turned[...], preferred_element_type=jnp.float32)
    scores = (both[:rows] + both[rows:]).astype(scores_ref.dtype)
    for block, place in enumerate(places):
        scores_ref[place] = scores[block * examples : (block + 1) * examples]


def module_scores(grads, fisher, query, places):
    slots, examples, size = grads.shape
    rows, queries = slots * examples, query.shape[1]
    return pl.pallas_call(
        functools.partial(score_kernel, places),
        out_shape=jax.ShapeDtypeStruct((slots, examples, queries), jnp.bfloat16),
        in_specs=[pl.BlockSpec(memory_space=pltpu.VMEM)] * 3,
        out_specs=pl.BlockSpec(memory_space=pltpu.VMEM),
        scratch_shapes=[
            pltpu.VMEM((rows, size), jnp.bfloat16),
            pltpu.VMEM((size, queries), jnp.bfloat16),
            pltpu.VMEM((2 * rows, size), jnp.bfloat16),
        ],
        compiler_params=pltpu.CompilerParams(vmem_limit_bytes=24 << 20),
        cost_estimate=pl.CostEstimate(
            flops=2 * rows * (fisher.size + 2 * query.size),
            bytes_accessed=2 * (fisher.size + query.size),
            transcendentals=0,
        ),
    )(grads, fisher, query)


def local(inputs_proj, outputs_proj, lengths, owner, fisher_inv, query_grads):
    count = owner.shape[0]
    out, back = listed(count), listed_by_distance(count)
    routed = form_grads(inputs_proj, outputs_proj, lengths, owner)
    received = lax.all_to_all(routed, "mod", split_axis=0, concat_axis=0, axis_index_groups=[out], tiled=True)
    partial = module_scores(received, fisher_inv, query_grads, [back.index(device) for device in out])
    spread = lax.all_to_all(partial, "mod", split_axis=0, concat_axis=0, axis_index_groups=[back], tiled=True)
    return jnp.sum(spread.astype(jnp.float32), axis=0)


def solution(mesh):
    return jax.shard_map(
        local,
        mesh=mesh,
        in_specs=(
            P(("grp", "mod"), None, None),
            P(("grp", "mod"), None, None),
            P(("grp", "mod")),
            P(),
            P("mod", None, None),
            P("mod", None, None),
        ),
        out_specs=P(("grp", "mod"), None),
        check_vma=False,
    )
```
